32 devices in a mesh: row: 4 (over z), col: 8 (over y, x, core).
Axes of the slice: x: 2, y: 2, z: 4, core: 2. Of those that a mesh axis runs over, the one named last changes fastest.
Arguments:
- spectra: bfloat16 [1024, 32, 128], P(('row', 'col')), may hold values from -6 to 6
- pair_bins: int32 [1024, 1024], P('row', 'col'), may hold values from 0 to 255
- row_subs: int32 [4, 16], P('row'), may hold values from 0 to 31, as said below
- station_subs: int32 [1024, 8], replicated, may hold values from 0 to 31, as said below
- kernel: bfloat16 [32, 256, 256], replicated, may hold values from -0.375 to 0.375
Outputs:
- spectrum: float32 [32, 32, 256], P(('row', 'col'))
The draws below stay inside these ranges and needn't reach their ends.
Inputs may be any that keep to these rules, and one draw needn't show every extreme that they name: `row_subs`: each row lists 16 distinct subarrays; each subarray is listed for exactly two row blocks. `station_subs`: each station names 8 distinct subarrays, all listed in row_subs for the station's row block.
All inputs are finite; a program needn't handle non-finite values.
Results may differ from the reference program's by a relative error of at most 0.0039.
Values may be sent and summed in bfloat16 or wider, within the bound.
A program may use at most 64 MiB of HBM per device.

```python
import jax
import jax.numpy as jnp
from jax import lax

F = 32
WIN2 = 128
NBIN = 256
V = 256
MS = 8
STA = 1024
ROW_STA = 256
NSUB = 32
LS = 16
N_ROW = 4
N_COL = 8


def make_lists(key):
    shuffled = jax.random.permutation(jax.random.fold_in(key, 11), NSUB).astype(jnp.int32)
    half_list = LS // 2
    quarter = half_list // 4
    row_ids = jnp.arange(N_ROW, dtype=jnp.int32)[:, None]
    slot_ids = jnp.arange(LS, dtype=jnp.int32)[None, :]
    inner = slot_ids % half_list
    far_rows = jnp.where(inner < quarter, row_ids + N_ROW - 1, jnp.where(inner < 2 * quarter, row_ids + 1, row_ids + N_ROW // 2)) % N_ROW
    block_ids = jnp.where(slot_ids < half_list, row_ids, far_rows)
    places = block_ids * half_list + inner
    return shuffled[places]


def draw_row_subs(key, part):
    return make_lists(key)


def draw_station_subs(key, part):
    lists = make_lists(key)
    scores = jax.random.randint(jax.random.fold_in(key, 23), (STA, LS), 0, 1 << 20) * LS + jnp.arange(LS, dtype=jnp.int32)[None, :]
    order = jnp.argsort(-scores, axis=1)[:, :MS]
    owners = lists[jnp.arange(STA, dtype=jnp.int32) // ROW_STA]
    return jnp.take_along_axis(owners, order, axis=1).astype(jnp.int32)


def set_ends(drawn, rng, low, high):
    shape = drawn.shape
    index_at = [jax.random.randint(jax.random.fold_in(rng, axis), (), 0, shape[axis]) for axis in range(len(shape))]
    drawn = drawn.at[tuple(index_at)].set(low)
    longest = shape.index(max(shape))
    index_at[longest] = (index_at[longest] + 1) % shape[longest]
    return drawn.at[tuple(index_at)].set(high)


def steps_of(key, dims, cuts, least, largest):
    level, own = 1.0, jax.random.fold_in(key, 6)
    for position, blocks in cuts:
        heights = jnp.exp(jax.random.uniform(jax.random.fold_in(own, position), (blocks,), jnp.float32, least / len(cuts), largest / len(cuts)))
        level = level * jnp.repeat(heights, dims[position] // blocks).reshape([-1 if axis == position else 1 for axis in range(len(dims))])
    return level


def normal_values(rng, extent, spread, most, pieces=(), kind=jnp.bfloat16):
    drawn = jax.random.normal(rng, extent, jnp.float32) * spread
    if len(pieces) > 0:
        drawn = steps_of(rng, extent, pieces, -0.22, 0.18) * drawn
    return jnp.clip(drawn, min=-most, max=most).astype(kind)


def setup_inputs(seed: int = 0) -> dict:
    seeds = jax.random.split(jax.random.key(seed), 6)
    spectra = normal_values(seeds[0], (STA, F, WIN2), 1.0, 6.0, ((0, 32),))
    pair_bins = set_ends(jax.random.randint(seeds[1], (STA, STA), 0, NBIN), jax.random.fold_in(seeds[1], 1), 0, NBIN - 1).astype(jnp.int32)
    row_subs = draw_row_subs(jax.random.fold_in(seeds[5], 71), 0)
    station_subs = draw_station_subs(jax.random.fold_in(seeds[5], 71), 0)
    kernel = normal_values(seeds[4], (F, NBIN, V), NBIN ** -0.5, 0.375)
    return {"spectra": spectra, "pair_bins": pair_bins, "row_subs": row_subs, "station_subs": station_subs, "kernel": kernel}


def reference(spectra, pair_bins, row_subs, station_subs, kernel):
    stations = spectra.shape[0]
    shard_rows = stations // (N_ROW * N_COL)
    row_span = stations // N_ROW
    col_span = stations // N_COL
    slot_count = row_subs.shape[1]
    positions = jnp.arange(col_span, dtype=jnp.int32)
    bin_ids = jnp.arange(NBIN, dtype=jnp.int32)

    def one_block(running, block_index):
        row_block = block_index // N_COL
        col_group = block_index % N_COL
        row_first = (row_block * row_span).astype(jnp.int32)
        row_spectra = lax.dynamic_slice_in_dim(spectra, row_first, row_span, 0).astype(jnp.float32)
        col_ids = ((positions // shard_rows * N_COL + col_group) * shard_rows + positions % shard_rows).astype(jnp.int32)
        col_spectra = jnp.take(spectra, col_ids, axis=0).astype(jnp.float32)
        cross_spec = jnp.einsum('aft,jft->faj', row_spectra, col_spectra, precision=lax.Precision.HIGHEST)
        cross_spec = lax.optimization_barrier(cross_spec.astype(jnp.bfloat16)).astype(jnp.float32)
        bins_block = lax.dynamic_slice(pair_bins, (row_first, (col_group * col_span).astype(jnp.int32)), (row_span, col_span))
        slot_subs = lax.dynamic_index_in_dim(row_subs, row_block.astype(jnp.int32), 0, keepdims=False)
        row_members = lax.dynamic_slice_in_dim(station_subs, row_first, row_span, 0)
        col_members = jnp.take(station_subs, col_ids, axis=0)
        row_mask = jnp.any(row_members[None, :, :] == slot_subs[:, None, None], axis=2).astype(jnp.float32)
        col_mask = jnp.any(col_members[None, :, :] == slot_subs[:, None, None], axis=2).astype(jnp.float32)
        weighted = row_mask[:, None, :, None] * col_mask[:, None, None, :] * cross_spec[None]
        onehot = (bins_block.reshape(-1, 1) == bin_ids[None, :]).astype(jnp.float32)
        partial_value = jnp.dot(weighted.reshape(slot_count * F, row_span * col_span), onehot, precision=lax.Precision.HIGHEST)
        running = running.at[slot_subs].add(partial_value.reshape(slot_count, F, NBIN))
        return (running, None)
    start_sums = jnp.zeros((NSUB, F, NBIN), jnp.float32)
    binned_sum, unused = lax.scan(one_block, start_sums, jnp.arange(N_ROW * N_COL, dtype=jnp.int32))
    binned = lax.optimization_barrier(binned_sum.astype(jnp.bfloat16)).astype(jnp.float32)
    velocity_power = jnp.einsum('sfb,fbv->sfv', binned, kernel.astype(jnp.float32), precision=lax.Precision.HIGHEST)
    scale = lax.rsqrt(lax.optimization_barrier(jnp.mean(velocity_power * velocity_power, axis=2, keepdims=True)) + 1e-06)
    return velocity_power * scale
```

```python
import functools

import jax
import jax.numpy as jnp
from jax import lax
from jax.experimental import pallas as pl
from jax.experimental.pallas import tpu as pltpu
from jax.sharding import PartitionSpec as P

MESH = pl.DeviceIdType.MESH
NT = (((1,), (1,)), ((), ()))
NBIN = 256
LANES = 128
PACK = 16
X, Y, S = 0, 1, 2


def flip(c, bit):
    return c + bit - 2 * bit * lax.rem(lax.div(c, bit), 2)


def split(x, n):
    if n & (n - 1) == 0:
        return x >> (n.bit_length() - 1), x & (n - 1)
    return lax.div(x, n), lax.rem(x, n)


def body(rows, cols, x_ref, bins_ref, subs_ref, members_ref, kern_ref, out_ref,
         xv, xf, bv, mv, kern, rowbuf, colbuf, bsend, bt, mid, msend, mirror, mt,
         member, pmask, hot, cross0, cross1, w0, w1, acc, part, got1, spread, got2, ready, got3,
         in_sem, own_send, own_recv, fwd_send, fwd_recv, sib_send, sib_recv, col_send, col_recv,
         mid_send, mid_recv, mir_send, mir_recv, send1, recv1, send2, recv2, send3, recv3):
    r, c = lax.axis_index("row"), lax.axis_index("col")
    shard, freqs, _ = xv.shape
    span, width = bv.shape
    slots = subs_ref.shape[1]
    half = freqs // 2
    quarter = half // 2
    share = half // cols
    tiles = span // LANES
    per_tile = LANES // shard
    units = rows + 1
    tree = cols == 8 and tiles == 2
    bf16, f32 = jnp.bfloat16, jnp.float32

    barrier = pltpu.get_barrier_semaphore()
    for d in range(1, rows):
        pl.semaphore_signal(barrier, inc=1, device_id=(lax.rem(r + d, rows), c), device_id_type=MESH)
    for d in range(1, cols):
        pl.semaphore_signal(barrier, inc=1, device_id=(r, lax.rem(c + d, cols)), device_id_type=MESH)
    loads = [pltpu.make_async_copy(bins_ref, bv, in_sem.at[0]),
             pltpu.make_async_copy(x_ref, xv, in_sem.at[1]),
             pltpu.make_async_copy(members_ref, mv, in_sem.at[2])]
    fetches = [pltpu.make_async_copy(kern_ref.at[pl.ds(q * half + c * share, share)], kern.at[q], in_sem.at[3 + q])
               for q in range(2)]
    for copy in loads + fetches:
        copy.start()

    loads[0].wait()
    ids = bv[...].astype(f32)
    bsend[...] = ids.astype(bf16)
    mine = pl.ds(pl.multiple_of(c * shard, shard), shard)
    mid[c] = bsend[mine, :]
    loads[1].wait()
    xf[...] = xv[...].astype(f32).reshape(shard * freqs, xv.shape[2])
    for f in range(freqs):
        block = xf[pl.ds(f, shard, stride=freqs), :].astype(bf16)
        rowbuf[f, mine, :] = block
        if f < half:
            colbuf[r, f] = block
        else:
            colbuf[rows, f - half] = block

    def mid_copy(d):
        to = lax.rem(c + d, cols)
        return pltpu.make_async_remote_copy(
            bsend.at[pl.ds(pl.multiple_of(to * shard, shard), shard), :], mid.at[c], mid_send.at[d], mid_recv.at[d],
            device_id=(r, to), device_id_type=MESH)

    def mir_copy(d):
        to = lax.rem(r + d, rows)
        return pltpu.make_async_remote_copy(
            msend.at[to], mirror.at[r], mir_send.at[d], mir_recv.at[d], device_id=(to, c), device_id_type=MESH)

    def slot(index, q):
        return rowbuf.at[pl.ds(q * half, half), pl.ds(pl.multiple_of(index * shard, shard), shard), :]

    bits = (2, 4, 1)

    def own_copy(way, q):
        return pltpu.make_async_remote_copy(
            slot(c, q), slot(c, q), own_send.at[way, q], own_recv.at[way, q],
            device_id=(r, flip(c, bits[way])), device_id_type=MESH)

    def fwd_copy(q):
        source = flip(c, bits[X] if q == 0 else bits[Y])
        return pltpu.make_async_remote_copy(
            slot(source, q), slot(source, q), fwd_send.at[q], fwd_recv.at[q],
            device_id=(r, flip(c, bits[Y] if q == 0 else bits[X])), device_id_type=MESH)

    def sib_copy(k, q):
        source = (flip(c, 2), flip(c, 4), flip(flip(c, 2), 4))[k]
        return pltpu.make_async_remote_copy(
            slot(source, q), slot(source, q), sib_send.at[k, q], sib_recv.at[k, q],
            device_id=(r, flip(c, 1)), device_id_type=MESH)

    def direct_copy(d):
        place = rowbuf.at[:, mine, :]
        return pltpu.make_async_remote_copy(
            place, place, own_send.at[d, 0], own_recv.at[d, 0],
            device_id=(r, lax.rem(c + d, cols)), device_id_type=MESH)

    def col_copy(way, d, p):
        source = r - way * (d - 1)
        there = r + way
        at = lax.rem(source + rows, rows)
        if d == 1 and way > 0:
            at = rows
        place = colbuf.at[at, pl.ds(p * quarter, quarter)]
        target = colbuf.at[lax.rem(source + rows, rows), pl.ds(p * quarter, quarter)]
        i = (way + 1) // 2
        return (there >= 0) & (there < rows) & (source >= 0) & (source < rows), pltpu.make_async_remote_copy(
            place, target, col_send.at[i, d, p], col_recv.at[i, d, p],
            device_id=(lax.rem(there + rows, rows), c), device_id_type=MESH)

    def col_start(way, d, p):
        made = col_copy(way, d, p)
        pl.when(made[0])(made[1].start)

    def col_wait(way, d, p):
        source = r - way * d

        @pl.when((source >= 0) & (source < rows))
        def _():
            place = colbuf.at[lax.rem(source + rows, rows), pl.ds(p * quarter, quarter)]
            i = (way + 1) // 2
            pltpu.make_async_remote_copy(
                place, place, col_send.at[i, d, p], col_recv.at[i, d, p],
                device_id=(lax.rem(r + way + rows, rows), c), device_id_type=MESH).wait_recv()

    def col_pass(d):
        for p in range(2):
            for way in (1, -1):
                col_wait(way, d, p)
                if d < rows - 1:
                    col_start(way, d + 1, p)

    loads[2].wait()
    stations = mv.shape[1]
    sub_at = lax.broadcasted_iota(jnp.int32, (slots, stations), 0)
    slot_ids = jnp.zeros((slots, stations), jnp.int32)
    for s in range(slots):
        slot_ids = jnp.where(sub_at == s, subs_ref[0, s], slot_ids)
    found = jnp.zeros((slots, stations), f32)
    for m in range(mv.shape[0]):
        found = jnp.where(slot_ids == mv[m:m + 1, :], 1.0, found)
    member[...] = found
    name = lax.broadcasted_iota(jnp.int32, (stations, width), 0)
    block_id, inside = split(lax.broadcasted_iota(jnp.int32, (stations, width), 1), shard)
    picked = jnp.where(name == (block_id * cols + c) * shard + inside, 1.0, 0.0).astype(bf16)
    col_mask = jnp.dot(found.astype(bf16), picked, preferred_element_type=f32)
    row_mask = member[:, pl.ds(pl.multiple_of(r * span, span), span)]
    lane = lax.broadcasted_iota(jnp.int32, (slots, width), 1)
    for t in range(tiles):
        bt[t] = ids[t * LANES:(t + 1) * LANES].T

    pl.semaphore_wait(barrier, cols + rows - 2)

    for d in range(1, cols):
        mid_copy(d).start()
    for p in range(2):
        for way in (1, -1):
            col_start(way, 1, p)
    if tree:
        own_copy(X, 0).start()
        own_copy(Y, 1).start()
        own_copy(X, 1).start()
        own_copy(Y, 0).start()
        own_copy(S, 0).start()
        own_copy(S, 1).start()
    else:
        for d in range(1, cols):
            direct_copy(d).start()

    def mask_one(j, carry):
        hit = jnp.sum(jnp.where(lane == j, col_mask, 0.0), axis=1, keepdims=True)
        pmask[j] = (hit * row_mask).astype(bf16)
        return carry

    lax.fori_loop(0, width, mask_one, 0, unroll=8)

    low = lax.broadcasted_iota(jnp.int32, (PACK, LANES), 0).astype(f32)
    levels = [(low + g * PACK).astype(bf16) for g in range(NBIN // PACK)]
    one, zero = jnp.ones((PACK, LANES), bf16), jnp.zeros((PACK, LANES), bf16)

    def spread_row(ref, index, t):
        row = ref[t, pl.ds(index, 1), :]
        return jnp.broadcast_to(row, (PACK, LANES)).astype(bf16)

    def heat(block, twice):
        def step(j, carry):
            for t in range(tiles):
                here = spread_row(bt, block * shard + j, t)
                there = spread_row(mt, block * shard + j, t) if twice else None
                for g, level in enumerate(levels):
                    value = jnp.where(here == level, one, zero)
                    if twice:
                        value = value + jnp.where(there == level, one, zero)
                    hot[block * tiles + t, g * PACK:(g + 1) * PACK,
                        pl.ds(pl.multiple_of(j * LANES, LANES), LANES)] = value
            return carry
        lax.fori_loop(0, shard, step, 0, unroll=2)

    heat(r, False)

    for d in range(1, cols):
        mid_copy(d).wait_recv()
    group = lax.broadcasted_iota(jnp.int32, (shard, LANES), 1) // shard
    for t in range(tiles):
        held = [mid[t * per_tile + k].astype(f32) for k in range(per_tile)]
        for b in range(rows):
            total = jnp.zeros((shard, LANES), f32)
            for k in range(per_tile):
                shift = ((k - b) * shard) % LANES
                moved = pltpu.roll(held[k], shift, 1) if shift else held[k]
                total = jnp.where(group == k, moved, total)
            msend[b, :, t * LANES:(t + 1) * LANES] = total.astype(bf16)
    for d in range(1, rows):
        mir_copy(d).start()

    if tree:
        own_copy(X, 0).wait_recv()
        fwd_copy(0).start()
        sib_copy(X, 0).start()
        own_copy(Y, 1).wait_recv()
        fwd_copy(1).start()
        sib_copy(Y, 1).start()
    col_pass(1)
    if tree:
        own_copy(X, 1).wait_recv()
        sib_copy(X, 1).start()
        own_copy(Y, 0).wait_recv()
        sib_copy(Y, 0).start()
    for d in range(2, rows - 1):
        col_pass(d)
    for d in range(1, rows):
        mir_copy(d).wait_recv()
    for b in range(rows):
        @pl.when(b != r)
        def _():
            for t in range(tiles):
                mt[t, b * shard:(b + 1) * shard, :] = mirror[b, :, t * LANES:(t + 1) * LANES].astype(f32)

    def heat_rest(k, carry):
        heat(lax.rem(r + 1 + k, rows), True)
        return carry

    lax.fori_loop(0, rows - 1, heat_rest, 0)

    if tree:
        own_copy(S, 0).wait_recv()
        own_copy(S, 1).wait_recv()
        sib_copy(X, 0).wait_recv()
        sib_copy(X, 1).wait_recv()
    else:
        for d in range(1, cols):
            direct_copy(d).wait_recv()
    own_tile = lax.div(c, per_tile)
    near = lax.min(r, rows - 1 - r)
    upward = jnp.where(r < rows - 1 - r, 1, -1)

    def unit_of(m):
        t, u = lax.div(m, units), lax.rem(m, units)
        tile = lax.rem(own_tile + t, tiles)
        k = lax.max(u - 2, 0)
        paired = k < 2 * near
        way = jnp.where(paired, 1 - 2 * lax.rem(k, 2), upward)
        dist = jnp.where(paired, lax.div(k, 2) + 1, k - near + 1)
        other = r + way * dist
        block = jnp.where(u < 2, r, other)
        q = jnp.where(u < 2, u, jnp.where(way > 0, 0, 1))
        at = jnp.where(u == 1, rows, block)
        return tile, block, q, at

    def need(m):
        @pl.when(m == units - 1)
        def _():
            for p in range(2):
                for way in (1, -1):
                    col_wait(way, rows - 1, p)

        if tree:
            @pl.when(m == 2)
            def _():
                fwd_copy(0).wait_recv()
                sib_copy(2, 0).start()
                fwd_copy(1).wait_recv()
                sib_copy(2, 1).start()

            @pl.when(m == units)
            def _():
                for k in (1, 2):
                    for q in range(2):
                        sib_copy(k, q).wait_recv()

    def build(m, cross, w):
        tile, block, q, at = unit_of(m)
        lanes = pl.ds(pl.multiple_of(tile * LANES, LANES), LANES)
        for f in range(half):
            cross[f * shard:(f + 1) * shard, :] = lax.dot_general(
                colbuf[at, f], rowbuf[q * half + f, lanes, :], NT, preferred_element_type=f32)
        for j in range(shard):
            mask = pmask[block * shard + j, :, lanes]
            for f in range(half):
                value = jnp.broadcast_to(cross[f * shard + j:f * shard + j + 1, :], (slots, LANES)).astype(bf16)
                w[f * slots:(f + 1) * slots, j * LANES:(j + 1) * LANES] = mask * value

    def multiply(m, w):
        tile, block, q, at = unit_of(m)
        acc[q] += lax.dot_general(w[...], hot[block * tiles + tile], NT, preferred_element_type=f32)

    acc[...] = jnp.zeros_like(acc)
    steps = tiles * units
    build(0, cross0, w0)

    def two(i, carry):
        need(2 * i + 1)
        need(2 * i + 2)
        build(2 * i + 1, cross1, w1)
        multiply(2 * i, w0)
        build(2 * i + 2, cross0, w0)
        multiply(2 * i + 1, w1)
        return carry

    lax.fori_loop(0, steps // 2 - 1, two, 0)
    need(steps - 1)
    build(steps - 1, cross1, w1)
    multiply(steps - 2, w0)
    multiply(steps - 1, w1)

    depth = share * slots

    def copy1(d):
        to = lax.rem(c + d, cols)
        return pltpu.make_async_remote_copy(
            part.at[to], got1.at[d], send1.at[d], recv1.at[d], device_id=(r, to), device_id_type=MESH)

    for k in range(cols):
        for q in range(2):
            part[k, q * depth:(q + 1) * depth, :] = acc[q, k * depth:(k + 1) * depth, :].astype(bf16)
    for d in range(1, cols):
        copy1(d).start()

    size = 2 * share * cols
    shape = (rows * size, 2 * depth)
    owner, tail = split(lax.broadcasted_iota(jnp.int32, shape, 0), size)
    fid, sid = split(tail, cols)
    fin, place = split(lax.broadcasted_iota(jnp.int32, shape, 1), slots)
    listed = jnp.zeros(shape, jnp.int32)
    for s in range(slots):
        listed = jnp.where(place == s, subs_ref[0, s], listed)
    chosen = jnp.where((owner * cols + sid == listed) & (fid == fin), 1.0, 0.0).astype(bf16)

    def copy2(d):
        to = lax.rem(r + d, rows)
        return pltpu.make_async_remote_copy(
            spread.at[to], got2.at[d], send2.at[d], recv2.at[d], device_id=(to, c), device_id_type=MESH)

    total = part[c].astype(f32)
    for d in range(1, cols):
        copy1(d).wait_recv()
        total = total + got1[d].astype(f32)
    spread[...] = jnp.dot(chosen, total.astype(bf16), preferred_element_type=f32).astype(bf16).reshape(rows, size, NBIN)
    for d in range(1, rows):
        copy2(d).start()
    for copy in fetches:
        copy.wait()
    total = spread[r].astype(f32)
    for d in range(1, rows):
        copy2(d).wait_recv()
        total = total + got2[d].astype(f32)
    for q in range(2):
        for f in range(share):
            n = q * share + f
            power = jnp.dot(total[n * cols:(n + 1) * cols].astype(bf16), kern[q, f], preferred_element_type=f32)
            power = power * lax.rsqrt(jnp.mean(power * power, axis=1, keepdims=True) + 1e-06)
            for k in range(cols):
                ready[k, n:n + 1, :] = power[k:k + 1]

    def copy3(d):
        to = lax.rem(c + d, cols)
        return pltpu.make_async_remote_copy(
            ready.at[to], got3.at[d], send3.at[d], recv3.at[d], device_id=(r, to), device_id_type=MESH)

    def put(source, block):
        for q in range(2):
            for f in range(share):
                out_ref[0, pl.ds(q * half + source * share + f, 1), :] = block[q * share + f:q * share + f + 1]

    for d in range(1, cols):
        copy3(d).start()
    put(c, ready[c])
    for d in range(1, cols):
        copy3(d).wait_recv()
        put(lax.rem(c - d + cols, cols), got3[d])
    for d in range(1, cols):
        mid_copy(d).wait_send()
        copy1(d).wait_send()
        copy3(d).wait_send()
    for d in range(1, rows):
        mir_copy(d).wait_send()
        copy2(d).wait_send()
        for p in range(2):
            for way in (1, -1):
                made = col_copy(way, d, p)
                pl.when(made[0])(made[1].wait_send)
    if tree:
        for q in range(2):
            for k in range(3):
                own_copy(k, q).wait_send()
                sib_copy(k, q).wait_send()
            fwd_copy(q).wait_send()
    else:
        for d in range(1, cols):
            direct_copy(d).wait_send()


def on_device(spectra, pair_bins, row_subs, station_subs, kernel):
    shard, freqs, width = spectra.shape
    rows, cols = lax.axis_size("row"), lax.axis_size("col")
    span, group = pair_bins.shape
    slots = row_subs.shape[1]
    half = freqs // 2
    share = half // cols
    depth = share * slots
    size = 2 * share * cols
    speeds = kernel.shape[2]
    tiles = span // LANES
    dma = pltpu.SemaphoreType.DMA
    bf16, f32 = jnp.bfloat16, jnp.float32
    hbm = pl.BlockSpec(memory_space=pl.ANY)
    return pl.pallas_call(
        functools.partial(body, rows, cols),
        out_shape=jax.ShapeDtypeStruct((1, freqs, speeds), f32),
        in_specs=[hbm, hbm, pl.BlockSpec(memory_space=pltpu.SMEM), hbm, hbm],
        out_specs=pl.BlockSpec(memory_space=pltpu.VMEM),
        scratch_shapes=[
            pltpu.VMEM(spectra.shape, bf16),
            pltpu.VMEM((shard * freqs, width), f32),
            pltpu.VMEM((span, group), jnp.int32),
            pltpu.VMEM((station_subs.shape[1], station_subs.shape[0]), jnp.int32),
            pltpu.VMEM((2, share, NBIN, speeds), bf16),
            pltpu.VMEM((freqs, cols * shard, width), bf16),
            pltpu.VMEM((rows + 1, half, shard, width), bf16),
            pltpu.VMEM((span, group), bf16),
            pltpu.VMEM((tiles, group, LANES), f32),
            pltpu.VMEM((cols, shard, group), bf16),
            pltpu.VMEM((rows, shard, span), bf16),
            pltpu.VMEM((rows, shard, span), bf16),
            pltpu.VMEM((tiles, group, LANES), f32),
            pltpu.VMEM((slots, station_subs.shape[0]), f32),
            pltpu.VMEM((group, slots, span), bf16),
            pltpu.VMEM((rows * tiles, NBIN, shard * LANES), bf16),
            pltpu.VMEM((half * shard, LANES), f32),
            pltpu.VMEM((half * shard, LANES), f32),
            pltpu.VMEM((half * slots, shard * LANES), bf16),
            pltpu.VMEM((half * slots, shard * LANES), bf16),
            pltpu.VMEM((2, half * slots, NBIN), f32),
            pltpu.VMEM((cols, 2 * depth, NBIN), bf16),
            pltpu.VMEM((cols, 2 * depth, NBIN), bf16),
            pltpu.VMEM((rows, size, NBIN), bf16),
            pltpu.VMEM((rows, size, NBIN), bf16),
            pltpu.VMEM((cols, 2 * share, speeds), f32),
            pltpu.VMEM((cols, 2 * share, speeds), f32),
            dma((5,)),
            dma((cols, 2)), dma((cols, 2)), dma((2,)), dma((2,)), dma((3, 2)), dma((3, 2)),
            dma((2, rows, 2)), dma((2, rows, 2)),
            dma((cols,)), dma((cols,)), dma((rows,)), dma((rows,)),
            dma((cols,)), dma((cols,)), dma((rows,)), dma((rows,)), dma((cols,)), dma((cols,)),
        ],
        compiler_params=pltpu.CompilerParams(collective_id=0, has_side_effects=True, vmem_limit_bytes=62 << 20),
        name="dispersion",
    )(spectra, pair_bins, row_subs, station_subs.T, kernel)


def solution(mesh):
    in_specs = (P(("row", "col"), None, None), P("row", "col"), P("row", None), P(), P())
    out_specs = P(("row", "col"), None, None)
    return jax.shard_map(
        on_device, mesh=mesh, in_specs=in_specs, out_specs=out_specs, check_vma=False
    )
```

```python
import functools

import jax
import jax.numpy as jnp
from jax import lax
from jax.experimental import pallas as pl
from jax.experimental.pallas import tpu as pltpu
from jax.sharding import PartitionSpec as P

MESH = pl.DeviceIdType.MESH
NT = (((1,), (1,)), ((), ()))
NBIN = 256
LANES = 128
PACK = 16
X, Y, S = 0, 1, 2


def flip(c, bit):
    return c + bit - 2 * bit * lax.rem(lax.div(c, bit), 2)


def split(x, n):
    if n & (n - 1) == 0:
        return x >> (n.bit_length() - 1), x & (n - 1)
    return lax.div(x, n), lax.rem(x, n)


def body(rows, cols, x_ref, bins_ref, subs_ref, members_ref, kern_ref, out_ref,
         xv, xf, bv, mv, kern, rowbuf, colbuf, bsend, bt, mid, msend, mirror, mt,
         member, pmask, hot0, hot1, cross0, cross1, w0, w1, acc, part, got1, spread, got2, ready, got3,
         in_sem, own_send, own_recv, fwd_send, fwd_recv, sib_send, sib_recv, col_send, col_recv,
         mid_send, mid_recv, mir_send, mir_recv, send1, recv1, send2, recv2, send3, recv3):
    r, c = lax.axis_index("row"), lax.axis_index("col")
    shard, freqs, _ = xv.shape
    span, width = bv.shape
    slots = subs_ref.shape[1]
    half = freqs // 2
    quarter = half // 2
    share = half // cols
    tiles = span // LANES
    per_tile = LANES // shard
    units = rows + 1
    tree = cols == 8 and tiles == 2
    own_tile = lax.div(c, per_tile)
    steps = rows + (tiles - 1) * (rows - 1) + tiles
    qa = jnp.where(2 * r < rows, 0, 1)
    qb = 1 - qa
    bf16, f32 = jnp.bfloat16, jnp.float32

    barrier = pltpu.get_barrier_semaphore()
    for d in range(1, rows):
        pl.semaphore_signal(barrier, inc=1, device_id=(lax.rem(r + d, rows), c), device_id_type=MESH)
    for d in range(1, cols):
        pl.semaphore_signal(barrier, inc=1, device_id=(r, lax.rem(c + d, cols)), device_id_type=MESH)
    loads = [pltpu.make_async_copy(bins_ref, bv, in_sem.at[0]),
             pltpu.make_async_copy(x_ref, xv, in_sem.at[1]),
             pltpu.make_async_copy(members_ref, mv, in_sem.at[2])]
    fetches = [pltpu.make_async_copy(kern_ref.at[pl.ds(q * half + c * share, share)], kern.at[q], in_sem.at[3 + q])
               for q in range(2)]
    for copy in loads + fetches:
        copy.start()

    loads[0].wait()
    ids = bv[...].astype(f32)
    bsend[...] = ids.astype(bf16)
    mine = pl.ds(pl.multiple_of(c * shard, shard), shard)
    mid[c] = bsend[mine, :]
    loads[1].wait()
    xf[...] = xv[...].astype(f32).reshape(shard * freqs, xv.shape[2])
    for f in range(freqs):
        block = xf[pl.ds(f, shard, stride=freqs), :].astype(bf16)
        rowbuf[f, mine, :] = block
        if f < half:
            colbuf[r, f] = block
        else:
            colbuf[rows, f - half] = block

    def mid_copy(d):
        to = lax.rem(c + d, cols)
        return pltpu.make_async_remote_copy(
            bsend.at[pl.ds(pl.multiple_of(to * shard, shard), shard), :], mid.at[c], mid_send.at[d], mid_recv.at[d],
            device_id=(r, to), device_id_type=MESH)

    def mir_copy(d):
        to = lax.rem(r + d, rows)
        return pltpu.make_async_remote_copy(
            msend.at[to], mirror.at[r], mir_send.at[d], mir_recv.at[d], device_id=(to, c), device_id_type=MESH)

    def slot(index, q):
        return rowbuf.at[pl.ds((qb if q else qa) * half, half), pl.ds(pl.multiple_of(index * shard, shard), shard), :]

    bits = (2, 4, 1)

    def own_copy(way, q):
        return pltpu.make_async_remote_copy(
            slot(c, q), slot(c, q), own_send.at[way, q], own_recv.at[way, q],
            device_id=(r, flip(c, bits[way])), device_id_type=MESH)

    def fwd_copy(q):
        source = flip(c, bits[X] if q == 0 else bits[Y])
        return pltpu.make_async_remote_copy(
            slot(source, q), slot(source, q), fwd_send.at[q], fwd_recv.at[q],
            device_id=(r, flip(c, bits[Y] if q == 0 else bits[X])), device_id_type=MESH)

    def sib_copy(k, q):
        source = (flip(c, 2), flip(c, 4), flip(flip(c, 2), 4))[k]
        return pltpu.make_async_remote_copy(
            slot(source, q), slot(source, q), sib_send.at[k, q], sib_recv.at[k, q],
            device_id=(r, flip(c, 1)), device_id_type=MESH)

    def direct_copy(d):
        place = rowbuf.at[:, mine, :]
        return pltpu.make_async_remote_copy(
            place, place, own_send.at[d, 0], own_recv.at[d, 0],
            device_id=(r, lax.rem(c + d, cols)), device_id_type=MESH)

    def col_copy(way, d, p):
        source = r - way * (d - 1)
        there = r + way
        at = lax.rem(source + rows, rows)
        if d == 1 and way > 0:
            at = rows
        place = colbuf.at[at, pl.ds(p * quarter, quarter)]
        target = colbuf.at[lax.rem(source + rows, rows), pl.ds(p * quarter, quarter)]
        i = (way + 1) // 2
        return (there >= 0) & (there < rows) & (source >= 0) & (source < rows), pltpu.make_async_remote_copy(
            place, target, col_send.at[i, d, p], col_recv.at[i, d, p],
            device_id=(lax.rem(there + rows, rows), c), device_id_type=MESH)

    def col_start(way, d, p):
        made = col_copy(way, d, p)
        pl.when(made[0])(made[1].start)

    def col_wait(way, d, p):
        source = r - way * d

        @pl.when((source >= 0) & (source < rows))
        def _():
            place = colbuf.at[lax.rem(source + rows, rows), pl.ds(p * quarter, quarter)]
            i = (way + 1) // 2
            pltpu.make_async_remote_copy(
                place, place, col_send.at[i, d, p], col_recv.at[i, d, p],
                device_id=(lax.rem(r + way + rows, rows), c), device_id_type=MESH).wait_recv()

    def col_pass(d):
        for p in range(2):
            for way in (1, -1):
                col_wait(way, d, p)
                if d < rows - 1:
                    col_start(way, d + 1, p)

    loads[2].wait()
    stations = mv.shape[1]
    sub_at = lax.broadcasted_iota(jnp.int32, (slots, stations), 0)
    slot_ids = jnp.zeros((slots, stations), jnp.int32)
    for s in range(slots):
        slot_ids = jnp.where(sub_at == s, subs_ref[0, s], slot_ids)
    found = jnp.zeros((slots, stations), f32)
    for m in range(mv.shape[0]):
        found = jnp.where(slot_ids == mv[m:m + 1, :], 1.0, found)
    member[...] = found
    name = lax.broadcasted_iota(jnp.int32, (stations, width), 0)
    block_id, inside = split(lax.broadcasted_iota(jnp.int32, (stations, width), 1), shard)
    picked = jnp.where(name == (block_id * cols + c) * shard + inside, 1.0, 0.0).astype(bf16)
    col_mask = jnp.dot(found.astype(bf16), picked, preferred_element_type=f32)
    row_mask = member[:, pl.ds(pl.multiple_of(r * span, span), span)]
    lane = lax.broadcasted_iota(jnp.int32, (slots, width), 1)
    for t in range(tiles):
        bt[t] = ids[t * LANES:(t + 1) * LANES].T

    pl.semaphore_wait(barrier, cols + rows - 2)

    for d in range(1, cols):
        mid_copy(d).start()
    for p in range(2):
        for way in (1, -1):
            col_start(way, 1, p)
    if tree:
        own_copy(X, 0).start()
        own_copy(Y, 1).start()
        own_copy(X, 1).start()
        own_copy(Y, 0).start()
        own_copy(S, 0).start()
        own_copy(S, 1).start()
    else:
        for d in range(1, cols):
            direct_copy(d).start()

    def bring(k, q):
        own_copy(k, q).wait_recv()
        if k == (X, Y)[q]:
            fwd_copy(q).start()
        sib_copy(k, q).start()

    def mask_one(j, carry):
        hit = jnp.sum(jnp.where(lane == j, col_mask, 0.0), axis=1, keepdims=True)
        pmask[j] = (hit * row_mask).astype(bf16)
        return carry

    lax.fori_loop(0, width, mask_one, 0, unroll=8)

    low = lax.broadcasted_iota(jnp.int32, (PACK, LANES), 0).astype(f32)
    levels = [(low + g * PACK).astype(bf16) for g in range(NBIN // PACK)]
    one, zero = jnp.ones((PACK, LANES), bf16), jnp.zeros((PACK, LANES), bf16)

    def spread_row(ref, index, t):
        row = ref[t, pl.ds(index, 1), :]
        return jnp.broadcast_to(row, (PACK, LANES)).astype(bf16)

    for d in range(1, cols):
        mid_copy(d).wait_recv()
    group = lax.broadcasted_iota(jnp.int32, (shard, LANES), 1) // shard
    for t in range(tiles):
        held = [mid[t * per_tile + k].astype(f32) for k in range(per_tile)]
        for b in range(rows):
            total = jnp.zeros((shard, LANES), f32)
            for k in range(per_tile):
                shift = ((k - b) * shard) % LANES
                moved = pltpu.roll(held[k], shift, 1) if shift else held[k]
                total = jnp.where(group == k, moved, total)
            msend[b, :, t * LANES:(t + 1) * LANES] = total.astype(bf16)
        mt[t, pl.ds(pl.multiple_of(r * shard, shard), shard), :] = jnp.where(
            own_tile == t, -1.0, msend[r, :, t * LANES:(t + 1) * LANES].astype(f32))
    for d in range(1, rows):
        mir_copy(d).start()

    col_pass(1)
    if tree:
        bring(X, 0)
        bring(Y, 1)
        own_copy(S, 0).wait_recv()
        sib_copy(X, 0).wait_recv()
    else:
        for d in range(1, cols):
            direct_copy(d).wait_recv()
    near = lax.min(r, rows - 1 - r)
    upward = jnp.where(r < rows - 1 - r, 1, -1)

    def unit_of(m):
        far = m >= steps - tiles
        first = m < rows
        t = jnp.where(far, m - (steps - tiles), jnp.where(first, 0, 1 + lax.div(lax.max(m - rows, 0), rows - 1)))
        u = jnp.where(far, rows, jnp.where(first, m, 1 + lax.rem(lax.max(m - rows, 0), rows - 1)))
        tile = lax.rem(own_tile + t, tiles)
        k = lax.max(u - 2, 0)
        paired = k < 2 * near
        way = jnp.where(paired, 1 - 2 * lax.rem(k, 2), upward)
        dist = jnp.where(paired, lax.div(k, 2) + 1, k - near + 1)
        other = r + way * dist
        block = jnp.where(u < 2, r, other)
        own_q = jnp.where(t == 0, jnp.where(u == 0, qa, qb), jnp.where(own_tile < tile, 0, 1))
        q = jnp.where(u < 2, own_q, jnp.where(way > 0, 0, 1))
        at = jnp.where((u < 2) & (q == 1), rows, block)
        return tile, block, q, at

    def need(m):
        @pl.when(m == 1)
        def _():
            for d in range(2, rows - 1):
                col_pass(d)
            if tree:
                bring(Y, 0)
                bring(X, 1)
                own_copy(S, 1).wait_recv()
                sib_copy(X, 1).wait_recv()
            for d in range(1, rows):
                mir_copy(d).wait_recv()
            for b in range(rows):
                @pl.when(b != r)
                def _():
                    for t in range(tiles):
                        mt[t, b * shard:(b + 1) * shard, :] = mirror[b, :, t * LANES:(t + 1) * LANES].astype(f32)

        if tree:
            @pl.when(m == 3)
            def _():
                for q in range(2):
                    fwd_copy(q).wait_recv()
                    sib_copy(2, q).start()

            @pl.when(m == rows)
            def _():
                for k in (1, 2):
                    for q in range(2):
                        sib_copy(k, q).wait_recv()

        @pl.when(m == steps - tiles)
        def _():
            for p in range(2):
                for way in (1, -1):
                    col_wait(way, rows - 1, p)

    def build(m, cross, w, hot):
        tile, block, q, at = unit_of(m)
        lanes = pl.ds(pl.multiple_of(tile * LANES, LANES), LANES)
        for f in range(half):
            cross[f * shard:(f + 1) * shard, :] = lax.dot_general(
                colbuf[at, f], rowbuf[q * half + f, lanes, :], NT, preferred_element_type=f32)
        for j in range(shard):
            here = spread_row(bt, block * shard + j, tile)
            there = spread_row(mt, block * shard + j, tile)
            for g, level in enumerate(levels):
                hot[j, g * PACK:(g + 1) * PACK, :] = (
                    jnp.where(here == level, one, zero) + jnp.where(there == level, one, zero))
            mask = pmask[block * shard + j, :, lanes]
            for f in range(half):
                value = jnp.broadcast_to(cross[f * shard + j:f * shard + j + 1, :], (slots, LANES)).astype(bf16)
                w[j, f * slots:(f + 1) * slots, :] = mask * value

    def multiply(m, w, hot):
        q = unit_of(m)[2]
        left = jnp.concatenate([w[j] for j in range(shard)], axis=1)
        right = jnp.concatenate([hot[j] for j in range(shard)], axis=1)
        acc[q] += lax.dot_general(left, right, NT, preferred_element_type=f32)

    acc[...] = jnp.zeros_like(acc)
    build(0, cross0, w0, hot0)

    def two(i, carry):
        need(2 * i + 1)
        need(2 * i + 2)
        build(2 * i + 1, cross1, w1, hot1)
        multiply(2 * i, w0, hot0)
        build(2 * i + 2, cross0, w0, hot0)
        multiply(2 * i + 1, w1, hot1)
        return carry

    lax.fori_loop(0, (steps - 1) // 2, two, 0)
    if steps % 2 == 0:
        need(steps - 1)
        build(steps - 1, cross1, w1, hot1)
        multiply(steps - 2, w0, hot0)
        multiply(steps - 1, w1, hot1)
    else:
        multiply(steps - 1, w0, hot0)

    depth = share * slots

    def copy1(d):
        to = lax.rem(c + d, cols)
        return pltpu.make_async_remote_copy(
            part.at[to], got1.at[d], send1.at[d], recv1.at[d], device_id=(r, to), device_id_type=MESH)

    for k in range(cols):
        for q in range(2):
            part[k, q * depth:(q + 1) * depth, :] = acc[q, k * depth:(k + 1) * depth, :].astype(bf16)
    for d in range(1, cols):
        copy1(d).start()

    size = 2 * share * cols
    shape = (rows * size, 2 * depth)
    owner, tail = split(lax.broadcasted_iota(jnp.int32, shape, 0), size)
    fid, sid = split(tail, cols)
    fin, place = split(lax.broadcasted_iota(jnp.int32, shape, 1), slots)
    listed = jnp.zeros(shape, jnp.int32)
    for s in range(slots):
        listed = jnp.where(place == s, subs_ref[0, s], listed)
    chosen = jnp.where((owner * cols + sid == listed) & (fid == fin), 1.0, 0.0).astype(bf16)

    def copy2(d):
        to = lax.rem(r + d, rows)
        return pltpu.make_async_remote_copy(
            spread.at[to], got2.at[d], send2.at[d], recv2.at[d], device_id=(to, c), device_id_type=MESH)

    total = part[c].astype(f32)
    for d in range(1, cols):
        copy1(d).wait_recv()
        total = total + got1[d].astype(f32)
    spread[...] = jnp.dot(chosen, total.astype(bf16), preferred_element_type=f32).astype(bf16).reshape(rows, size, NBIN)
    for d in range(1, rows):
        copy2(d).start()
    for copy in fetches:
        copy.wait()
    total = spread[r].astype(f32)
    for d in range(1, rows):
        copy2(d).wait_recv()
        total = total + got2[d].astype(f32)
    for q in range(2):
        for f in range(share):
            n = q * share + f
            power = jnp.dot(total[n * cols:(n + 1) * cols].astype(bf16), kern[q, f], preferred_element_type=f32)
            power = power * lax.rsqrt(jnp.mean(power * power, axis=1, keepdims=True) + 1e-06)
            for k in range(cols):
                ready[k, n:n + 1, :] = power[k:k + 1]

    def copy3(d):
        to = lax.rem(c + d, cols)
        return pltpu.make_async_remote_copy(
            ready.at[to], got3.at[d], send3.at[d], recv3.at[d], device_id=(r, to), device_id_type=MESH)

    def put(source, block):
        for q in range(2):
            for f in range(share):
                out_ref[0, pl.ds(q * half + source * share + f, 1), :] = block[q * share + f:q * share + f + 1]

    for d in range(1, cols):
        copy3(d).start()
    put(c, ready[c])
    for d in range(1, cols):
        copy3(d).wait_recv()
        put(lax.rem(c - d + cols, cols), got3[d])
    for d in range(1, cols):
        mid_copy(d).wait_send()
        copy1(d).wait_send()
        copy3(d).wait_send()
    for d in range(1, rows):
        mir_copy(d).wait_send()
        copy2(d).wait_send()
        for p in range(2):
            for way in (1, -1):
                made = col_copy(way, d, p)
                pl.when(made[0])(made[1].wait_send)
    if tree:
        for q in range(2):
            for k in range(3):
                own_copy(k, q).wait_send()
                sib_copy(k, q).wait_send()
            fwd_copy(q).wait_send()
    else:
        for d in range(1, cols):
            direct_copy(d).wait_send()


def on_device(spectra, pair_bins, row_subs, station_subs, kernel):
    shard, freqs, width = spectra.shape
    rows, cols = lax.axis_size("row"), lax.axis_size("col")
    span, group = pair_bins.shape
    slots = row_subs.shape[1]
    half = freqs // 2
    share = half // cols
    depth = share * slots
    size = 2 * share * cols
    speeds = kernel.shape[2]
    tiles = span // LANES
    dma = pltpu.SemaphoreType.DMA
    bf16, f32 = jnp.bfloat16, jnp.float32
    hbm = pl.BlockSpec(memory_space=pl.ANY)
    return pl.pallas_call(
        functools.partial(body, rows, cols),
        out_shape=jax.ShapeDtypeStruct((1, freqs, speeds), f32),
        in_specs=[hbm, hbm, pl.BlockSpec(memory_space=pltpu.SMEM), hbm, hbm],
        out_specs=pl.BlockSpec(memory_space=pltpu.VMEM),
        scratch_shapes=[
            pltpu.VMEM(spectra.shape, bf16),
            pltpu.VMEM((shard * freqs, width), f32),
            pltpu.VMEM((span, group), jnp.int32),
            pltpu.VMEM((station_subs.shape[1], station_subs.shape[0]), jnp.int32),
            pltpu.VMEM((2, share, NBIN, speeds), bf16),
            pltpu.VMEM((freqs, cols * shard, width), bf16),
            pltpu.VMEM((rows + 1, half, shard, width), bf16),
            pltpu.VMEM((span, group), bf16),
            pltpu.VMEM((tiles, group, LANES), f32),
            pltpu.VMEM((cols, shard, group), bf16),
            pltpu.VMEM((rows, shard, span), bf16),
            pltpu.VMEM((rows, shard, span), bf16),
            pltpu.VMEM((tiles, group, LANES), f32),
            pltpu.VMEM((slots, station_subs.shape[0]), f32),
            pltpu.VMEM((group, slots, span), bf16),
            pltpu.VMEM((shard, NBIN, LANES), bf16),
            pltpu.VMEM((shard, NBIN, LANES), bf16),
            pltpu.VMEM((half * shard, LANES), f32),
            pltpu.VMEM((half * shard, LANES), f32),
            pltpu.VMEM((shard, half * slots, LANES), bf16),
            pltpu.VMEM((shard, half * slots, LANES), bf16),
            pltpu.VMEM((2, half * slots, NBIN), f32),
            pltpu.VMEM((cols, 2 * depth, NBIN), bf16),
            pltpu.VMEM((cols, 2 * depth, NBIN), bf16),
            pltpu.VMEM((rows, size, NBIN), bf16),
            pltpu.VMEM((rows, size, NBIN), bf16),
            pltpu.VMEM((cols, 2 * share, speeds), f32),
            pltpu.VMEM((cols, 2 * share, speeds), f32),
            dma((5,)),
            dma((cols, 2)), dma((cols, 2)), dma((2,)), dma((2,)), dma((3, 2)), dma((3, 2)),
            dma((2, rows, 2)), dma((2, rows, 2)),
            dma((cols,)), dma((cols,)), dma((rows,)), dma((rows,)),
            dma((cols,)), dma((cols,)), dma((rows,)), dma((rows,)), dma((cols,)), dma((cols,)),
        ],
        compiler_params=pltpu.CompilerParams(collective_id=0, has_side_effects=True, vmem_limit_bytes=62 << 20),
        name="dispersion",
    )(spectra, pair_bins, row_subs, station_subs.T, kernel)


def solution(mesh):
    in_specs = (P(("row", "col"), None, None), P("row", "col"), P("row", None), P(), P())
    out_specs = P(("row", "col"), None, None)
    return jax.shard_map(
        on_device, mesh=mesh, in_specs=in_specs, out_specs=out_specs, check_vma=False
    )
```

```python
import functools

import jax
import jax.numpy as jnp
from jax import lax
from jax.experimental import pallas as pl
from jax.experimental.pallas import tpu as pltpu
from jax.sharding import PartitionSpec as P

MESH = pl.DeviceIdType.MESH
NT = (((1,), (1,)), ((), ()))
NBIN = 256
LANES = 128
PACK = 16
X, Y, S = 0, 1, 2


def flip(c, bit):
    return c + bit - 2 * bit * lax.rem(lax.div(c, bit), 2)


def split(x, n):
    if n & (n - 1) == 0:
        return x >> (n.bit_length() - 1), x & (n - 1)
    return lax.div(x, n), lax.rem(x, n)


def body(rows, cols, x_ref, bins_ref, subs_ref, members_ref, kern_ref, out_ref,
         xv, xf, bv, mv, kern, rowbuf, colbuf, bsend, bt, mid, msend, mirror, mt,
         member, pmask, hot0, hot1, cross0, cross1, w0, w1, acc, part, got1, spread, got2, ready, got3,
         in_sem, own_send, own_recv, fwd_send, fwd_recv, sib_send, sib_recv, col_send, col_recv,
         mid_send, mid_recv, mir_send, mir_recv, send1, recv1, send2, recv2, send3, recv3):
    r, c = lax.axis_index("row"), lax.axis_index("col")
    shard, freqs, _ = xv.shape
    span, width = bv.shape
    slots = subs_ref.shape[1]
    half = freqs // 2
    quarter = half // 2
    share = half // cols
    tiles = span // LANES
    per_tile = LANES // shard
    units = rows + 1
    tree = cols == 8 and tiles == 2
    own_tile = lax.div(c, per_tile)
    steps = rows + (tiles - 1) * (rows - 1) + tiles
    qa = jnp.where(2 * r < rows, 0, 1)
    qb = 1 - qa
    bf16, f32 = jnp.bfloat16, jnp.float32

    barrier = pltpu.get_barrier_semaphore()
    for d in range(1, rows):
        pl.semaphore_signal(barrier, inc=1, device_id=(lax.rem(r + d, rows), c), device_id_type=MESH)
    for d in range(1, cols):
        pl.semaphore_signal(barrier, inc=1, device_id=(r, lax.rem(c + d, cols)), device_id_type=MESH)
    loads = [pltpu.make_async_copy(bins_ref, bv, in_sem.at[0]),
             pltpu.make_async_copy(x_ref, xv, in_sem.at[1]),
             pltpu.make_async_copy(members_ref, mv, in_sem.at[2])]
    fetches = [pltpu.make_async_copy(kern_ref.at[pl.ds(q * half + c * share, share)], kern.at[q], in_sem.at[3 + q])
               for q in range(2)]
    for copy in loads + fetches:
        copy.start()

    loads[0].wait()
    ids = bv[...].astype(f32)
    bsend[...] = ids.astype(bf16)
    mine = pl.ds(pl.multiple_of(c * shard, shard), shard)
    mid[c] = bsend[mine, :]
    loads[1].wait()
    xf[...] = xv[...].astype(f32).reshape(shard * freqs, xv.shape[2])
    for f in range(freqs):
        block = xf[pl.ds(f, shard, stride=freqs), :].astype(bf16)
        rowbuf[f, mine, :] = block
        if f < half:
            colbuf[r, f] = block
        else:
            colbuf[rows, f - half] = block

    def mid_copy(d):
        to = lax.rem(c + d, cols)
        return pltpu.make_async_remote_copy(
            bsend.at[pl.ds(pl.multiple_of(to * shard, shard), shard), :], mid.at[c], mid_send.at[d], mid_recv.at[d],
            device_id=(r, to), device_id_type=MESH)

    def mir_copy(d):
        to = lax.rem(r + d, rows)
        return pltpu.make_async_remote_copy(
            msend.at[to], mirror.at[r], mir_send.at[d], mir_recv.at[d], device_id=(to, c), device_id_type=MESH)

    def pick(q):
        return qb if q else qa

    def slot(index, q):
        return rowbuf.at[pl.ds(pick(q) * half, half), pl.ds(pl.multiple_of(index * shard, shard), shard), :]

    bits = (2, 4, 1)

    def own_copy(way, q):
        return pltpu.make_async_remote_copy(
            slot(c, q), slot(c, q), own_send.at[way, q], own_recv.at[way, q],
            device_id=(r, flip(c, bits[way])), device_id_type=MESH)

    def fwd_copy(q):
        source = flip(c, bits[X] if q == 0 else bits[Y])
        return pltpu.make_async_remote_copy(
            slot(source, q), slot(source, q), fwd_send.at[q], fwd_recv.at[q],
            device_id=(r, flip(c, bits[Y] if q == 0 else bits[X])), device_id_type=MESH)

    def sib_copy(k, q):
        source = (flip(c, 2), flip(c, 4), flip(flip(c, 2), 4))[k]
        return pltpu.make_async_remote_copy(
            slot(source, q), slot(source, q), sib_send.at[k, q], sib_recv.at[k, q],
            device_id=(r, flip(c, 1)), device_id_type=MESH)

    def direct_copy(d):
        place = rowbuf.at[:, mine, :]
        return pltpu.make_async_remote_copy(
            place, place, own_send.at[d, 0], own_recv.at[d, 0],
            device_id=(r, lax.rem(c + d, cols)), device_id_type=MESH)

    def col_copy(way, d, p):
        source = r - way * (d - 1)
        there = r + way
        at = lax.rem(source + rows, rows)
        if d == 1 and way > 0:
            at = rows
        place = colbuf.at[at, pl.ds(p * quarter, quarter)]
        target = colbuf.at[lax.rem(source + rows, rows), pl.ds(p * quarter, quarter)]
        i = (way + 1) // 2
        return (there >= 0) & (there < rows) & (source >= 0) & (source < rows), pltpu.make_async_remote_copy(
            place, target, col_send.at[i, d, p], col_recv.at[i, d, p],
            device_id=(lax.rem(there + rows, rows), c), device_id_type=MESH)

    def col_start(way, d, p):
        made = col_copy(way, d, p)
        pl.when(made[0])(made[1].start)

    def col_wait(way, d, p):
        source = r - way * d

        @pl.when((source >= 0) & (source < rows))
        def _():
            place = colbuf.at[lax.rem(source + rows, rows), pl.ds(p * quarter, quarter)]
            i = (way + 1) // 2
            pltpu.make_async_remote_copy(
                place, place, col_send.at[i, d, p], col_recv.at[i, d, p],
                device_id=(lax.rem(r + way + rows, rows), c), device_id_type=MESH).wait_recv()

    def col_pass(d):
        for p in range(2):
            for way in (1, -1):
                col_wait(way, d, p)
                if d < rows - 1:
                    col_start(way, d + 1, p)

    pl.semaphore_wait(barrier, cols + rows - 2)

    for d in range(1, cols):
        mid_copy(d).start()
    for p in range(2):
        for way in (1, -1):
            col_start(way, 1, p)
    if tree:
        own_copy(X, 0).start()
        own_copy(Y, 1).start()
        own_copy(X, 1).start()
        own_copy(Y, 0).start()
        own_copy(S, 0).start()
        own_copy(S, 1).start()
    else:
        for d in range(1, cols):
            direct_copy(d).start()

    loads[2].wait()
    stations = mv.shape[1]
    sub_at = lax.broadcasted_iota(jnp.int32, (slots, stations), 0)
    slot_ids = jnp.zeros((slots, stations), jnp.int32)
    for s in range(slots):
        slot_ids = jnp.where(sub_at == s, subs_ref[0, s], slot_ids)
    found = jnp.zeros((slots, stations), f32)
    for m in range(mv.shape[0]):
        found = jnp.where(slot_ids == mv[m:m + 1, :], 1.0, found)
    member[...] = found
    name = lax.broadcasted_iota(jnp.int32, (stations, width), 0)
    block_id, inside = split(lax.broadcasted_iota(jnp.int32, (stations, width), 1), shard)
    picked = jnp.where(name == (block_id * cols + c) * shard + inside, 1.0, 0.0).astype(bf16)
    col_mask = jnp.dot(found.astype(bf16), picked, preferred_element_type=f32)
    row_mask = member[:, pl.ds(pl.multiple_of(r * span, span), span)]
    lane = lax.broadcasted_iota(jnp.int32, (slots, width), 1)
    for t in range(tiles):
        bt[t] = ids[t * LANES:(t + 1) * LANES].T

    def bring(k, q):
        own_copy(k, q).wait_recv()
        if k == (X, Y)[q]:
            fwd_copy(q).start()
        sib_copy(k, q).start()

    def mask_one(j, carry):
        hit = jnp.sum(jnp.where(lane == j, col_mask, 0.0), axis=1, keepdims=True)
        pmask[j] = (hit * row_mask).astype(bf16)
        return carry

    lax.fori_loop(0, width, mask_one, 0, unroll=8)

    low = lax.broadcasted_iota(jnp.int32, (PACK, LANES), 0).astype(f32)
    levels = [(low + g * PACK).astype(bf16) for g in range(NBIN // PACK)]
    one, zero = jnp.ones((PACK, LANES), bf16), jnp.zeros((PACK, LANES), bf16)

    def spread_row(ref, index, t):
        row = ref[t, pl.ds(index, 1), :]
        return jnp.broadcast_to(row, (PACK, LANES)).astype(bf16)

    for d in range(1, cols):
        mid_copy(d).wait_recv()
    group = lax.broadcasted_iota(jnp.int32, (shard, LANES), 1) // shard
    for t in range(tiles):
        held = [mid[t * per_tile + k].astype(f32) for k in range(per_tile)]
        for b in range(rows):
            total = jnp.zeros((shard, LANES), f32)
            for k in range(per_tile):
                shift = ((k - b) * shard) % LANES
                moved = pltpu.roll(held[k], shift, 1) if shift else held[k]
                total = jnp.where(group == k, moved, total)
            msend[b, :, t * LANES:(t + 1) * LANES] = total.astype(bf16)
        mt[t, pl.ds(pl.multiple_of(r * shard, shard), shard), :] = jnp.where(
            own_tile == t, -1.0, msend[r, :, t * LANES:(t + 1) * LANES].astype(f32))
    for d in range(1, rows):
        mir_copy(d).start()

    col_pass(1)
    if tree:
        bring(X, 0)
        bring(Y, 1)
        own_copy(S, 0).wait_recv()
        sib_copy(X, 0).wait_recv()
    else:
        for d in range(1, cols):
            direct_copy(d).wait_recv()
    near = lax.min(r, rows - 1 - r)
    upward = jnp.where(r < rows - 1 - r, 1, -1)

    def unit_of(m):
        far = m >= steps - tiles
        first = m < rows
        t = jnp.where(far, m - (steps - tiles), jnp.where(first, 0, 1 + lax.div(lax.max(m - rows, 0), rows - 1)))
        u = jnp.where(far, rows, jnp.where(first, m, 1 + lax.rem(lax.max(m - rows, 0), rows - 1)))
        tile = lax.rem(own_tile + t, tiles)
        k = lax.max(u - 2, 0)
        paired = k < 2 * near
        way = jnp.where(paired, 1 - 2 * lax.rem(k, 2), upward)
        dist = jnp.where(paired, lax.div(k, 2) + 1, k - near + 1)
        other = r + way * dist
        block = jnp.where(u < 2, r, other)
        own_q = jnp.where(t == 0, jnp.where(u == 0, qa, qb), jnp.where(own_tile < tile, 0, 1))
        q = jnp.where(u < 2, own_q, jnp.where(way > 0, 0, 1))
        at = jnp.where((u < 2) & (q == 1), rows, block)
        return tile, block, q, at

    def need(m):
        if tree:
            @pl.when(m == 1)
            def _():
                bring(Y, 0)
                bring(X, 1)
                own_copy(S, 1).wait_recv()
                sib_copy(X, 1).wait_recv()

        @pl.when(m == 2)
        def _():
            for d in range(2, rows - 1):
                col_pass(d)
            for d in range(1, rows):
                mir_copy(d).wait_recv()
            for b in range(rows):
                @pl.when(b != r)
                def _():
                    for t in range(tiles):
                        mt[t, b * shard:(b + 1) * shard, :] = mirror[b, :, t * LANES:(t + 1) * LANES].astype(f32)

        if tree:
            @pl.when(m == rows)
            def _():
                for q in range(2):
                    fwd_copy(q).wait_recv()
                    sib_copy(2, q).start()
                for k in (1, 2):
                    for q in range(2):
                        sib_copy(k, q).wait_recv()

        @pl.when(m == steps - tiles)
        def _():
            for p in range(2):
                for way in (1, -1):
                    col_wait(way, rows - 1, p)

    def build(m, cross, w, hot):
        tile, block, q, at = unit_of(m)
        lanes = pl.ds(pl.multiple_of(tile * LANES, LANES), LANES)
        for f in range(half):
            cross[f * shard:(f + 1) * shard, :] = lax.dot_general(
                colbuf[at, f], rowbuf[q * half + f, lanes, :], NT, preferred_element_type=f32)
        for j in range(shard):
            here = spread_row(bt, block * shard + j, tile)
            there = spread_row(mt, block * shard + j, tile)
            for g, level in enumerate(levels):
                hot[j, g * PACK:(g + 1) * PACK, :] = (
                    jnp.where(here == level, one, zero) + jnp.where(there == level, one, zero))
            mask = pmask[block * shard + j, :, lanes]
            for f in range(half):
                value = jnp.broadcast_to(cross[f * shard + j:f * shard + j + 1, :], (slots, LANES)).astype(bf16)
                w[j, f * slots:(f + 1) * slots, :] = mask * value

    def multiply(m, w, hot):
        q = unit_of(m)[2]
        left = jnp.concatenate([w[j] for j in range(shard)], axis=1)
        right = jnp.concatenate([hot[j] for j in range(shard)], axis=1)
        acc[q] += lax.dot_general(left, right, NT, preferred_element_type=f32)

    acc[...] = jnp.zeros_like(acc)
    sets = ((cross0, w0, hot0), (cross1, w1, hot1))

    def advance(m, odd):
        build(m, *sets[odd])
        multiply(m - 1, *sets[1 - odd][1:])

    build(0, *sets[0])
    need(1)
    advance(1, 1)

    def two(i, carry):
        need(2 * i + 2)
        need(2 * i + 3)
        advance(2 * i + 2, 0)
        advance(2 * i + 3, 1)
        return carry

    depth = share * slots
    early = tiles == 2 and rows % 2 == 0

    def copy1(d, n):
        to = lax.rem(c + d, cols)
        return pltpu.make_async_remote_copy(
            part.at[to, pick(n)], got1.at[d, pick(n)], send1.at[d, n], recv1.at[d, n],
            device_id=(r, to), device_id_type=MESH)

    def hand_out(n):
        for k in range(cols):
            part[k, pick(n)] = acc[pick(n), k * depth:(k + 1) * depth, :].astype(bf16)
        for d in range(1, cols):
            copy1(d, n).start()

    paired = (steps - 2) // 2
    lax.fori_loop(0, paired, two, 0)
    if early:
        hand_out(1)
    if steps % 2:
        need(steps - 1)
        advance(steps - 1, 0)
    multiply(steps - 1, *sets[(steps - 1) % 2][1:])
    for n in range(1 if early else 2):
        hand_out(n)

    size = 2 * share * cols
    shape = (rows * size, 2 * depth)
    owner, tail = split(lax.broadcasted_iota(jnp.int32, shape, 0), size)
    fid, sid = split(tail, cols)
    fin, place = split(lax.broadcasted_iota(jnp.int32, shape, 1), slots)
    listed = jnp.zeros(shape, jnp.int32)
    for s in range(slots):
        listed = jnp.where(place == s, subs_ref[0, s], listed)
    chosen = jnp.where((owner * cols + sid == listed) & (fid == fin), 1.0, 0.0).astype(bf16)

    def copy2(d):
        to = lax.rem(r + d, rows)
        return pltpu.make_async_remote_copy(
            spread.at[to], got2.at[d], send2.at[d], recv2.at[d], device_id=(to, c), device_id_type=MESH)

    for n in (1, 0):
        for d in range(1, cols):
            copy1(d, n).wait_recv()
    total = part[c].astype(f32)
    for d in range(1, cols):
        total = total + got1[d].astype(f32)
    total = total.reshape(2 * depth, NBIN)
    spread[...] = jnp.dot(chosen, total.astype(bf16), preferred_element_type=f32).astype(bf16).reshape(rows, size, NBIN)
    for d in range(1, rows):
        copy2(d).start()
    for copy in fetches:
        copy.wait()
    total = spread[r].astype(f32)
    for d in range(1, rows):
        copy2(d).wait_recv()
        total = total + got2[d].astype(f32)
    for q in range(2):
        for f in range(share):
            n = q * share + f
            power = jnp.dot(total[n * cols:(n + 1) * cols].astype(bf16), kern[q, f], preferred_element_type=f32)
            power = power * lax.rsqrt(jnp.mean(power * power, axis=1, keepdims=True) + 1e-06)
            for k in range(cols):
                ready[k, n:n + 1, :] = power[k:k + 1]

    def copy3(d):
        to = lax.rem(c + d, cols)
        return pltpu.make_async_remote_copy(
            ready.at[to], got3.at[d], send3.at[d], recv3.at[d], device_id=(r, to), device_id_type=MESH)

    def put(source, block):
        for q in range(2):
            for f in range(share):
                out_ref[0, pl.ds(q * half + source * share + f, 1), :] = block[q * share + f:q * share + f + 1]

    for d in range(1, cols):
        copy3(d).start()
    put(c, ready[c])
    for d in range(1, cols):
        copy3(d).wait_recv()
        put(lax.rem(c - d + cols, cols), got3[d])
    for d in range(1, cols):
        mid_copy(d).wait_send()
        copy1(d, 0).wait_send()
        copy1(d, 1).wait_send()
        copy3(d).wait_send()
    for d in range(1, rows):
        mir_copy(d).wait_send()
        copy2(d).wait_send()
        for p in range(2):
            for way in (1, -1):
                made = col_copy(way, d, p)
                pl.when(made[0])(made[1].wait_send)
    if tree:
        for q in range(2):
            for k in range(3):
                own_copy(k, q).wait_send()
                sib_copy(k, q).wait_send()
            fwd_copy(q).wait_send()
    else:
        for d in range(1, cols):
            direct_copy(d).wait_send()


def on_device(spectra, pair_bins, row_subs, station_subs, kernel):
    shard, freqs, width = spectra.shape
    rows, cols = lax.axis_size("row"), lax.axis_size("col")
    span, group = pair_bins.shape
    slots = row_subs.shape[1]
    half = freqs // 2
    share = half // cols
    depth = share * slots
    size = 2 * share * cols
    speeds = kernel.shape[2]
    tiles = span // LANES
    dma = pltpu.SemaphoreType.DMA
    bf16, f32 = jnp.bfloat16, jnp.float32
    hbm = pl.BlockSpec(memory_space=pl.ANY)
    return pl.pallas_call(
        functools.partial(body, rows, cols),
        out_shape=jax.ShapeDtypeStruct((1, freqs, speeds), f32),
        in_specs=[hbm, hbm, pl.BlockSpec(memory_space=pltpu.SMEM), hbm, hbm],
        out_specs=pl.BlockSpec(memory_space=pltpu.VMEM),
        scratch_shapes=[
            pltpu.VMEM(spectra.shape, bf16),
            pltpu.VMEM((shard * freqs, width), f32),
            pltpu.VMEM((span, group), jnp.int32),
            pltpu.VMEM((station_subs.shape[1], station_subs.shape[0]), jnp.int32),
            pltpu.VMEM((2, share, NBIN, speeds), bf16),
            pltpu.VMEM((freqs, cols * shard, width), bf16),
            pltpu.VMEM((rows + 1, half, shard, width), bf16),
            pltpu.VMEM((span, group), bf16),
            pltpu.VMEM((tiles, group, LANES), f32),
            pltpu.VMEM((cols, shard, group), bf16),
            pltpu.VMEM((rows, shard, span), bf16),
            pltpu.VMEM((rows, shard, span), bf16),
            pltpu.VMEM((tiles, group, LANES), f32),
            pltpu.VMEM((slots, station_subs.shape[0]), f32),
            pltpu.VMEM((group, slots, span), bf16),
            pltpu.VMEM((shard, NBIN, LANES), bf16),
            pltpu.VMEM((shard, NBIN, LANES), bf16),
            pltpu.VMEM((half * shard, LANES), f32),
            pltpu.VMEM((half * shard, LANES), f32),
            pltpu.VMEM((shard, half * slots, LANES), bf16),
            pltpu.VMEM((shard, half * slots, LANES), bf16),
            pltpu.VMEM((2, half * slots, NBIN), f32),
            pltpu.VMEM((cols, 2, depth, NBIN), bf16),
            pltpu.VMEM((cols, 2, depth, NBIN), bf16),
            pltpu.VMEM((rows, size, NBIN), bf16),
            pltpu.VMEM((rows, size, NBIN), bf16),
            pltpu.VMEM((cols, 2 * share, speeds), f32),
            pltpu.VMEM((cols, 2 * share, speeds), f32),
            dma((5,)),
            dma((cols, 2)), dma((cols, 2)), dma((2,)), dma((2,)), dma((3, 2)), dma((3, 2)),
            dma((2, rows, 2)), dma((2, rows, 2)),
            dma((cols,)), dma((cols,)), dma((rows,)), dma((rows,)),
            dma((cols, 2)), dma((cols, 2)), dma((rows,)), dma((rows,)), dma((cols,)), dma((cols,)),
        ],
        compiler_params=pltpu.CompilerParams(collective_id=0, has_side_effects=True, vmem_limit_bytes=62 << 20),
        name="dispersion",
    )(spectra, pair_bins, row_subs, station_subs.T, kernel)


def solution(mesh):
    in_specs = (P(("row", "col"), None, None), P("row", "col"), P("row", None), P(), P())
    out_specs = P(("row", "col"), None, None)
    return jax.shard_map(
        on_device, mesh=mesh, in_specs=in_specs, out_specs=out_specs, check_vma=False
    )
```

```python
import functools

import jax
import jax.numpy as jnp
from jax import lax
from jax.experimental import pallas as pl
from jax.experimental.pallas import tpu as pltpu
from jax.sharding import PartitionSpec as P

MESH = pl.DeviceIdType.MESH
NT = (((1,), (1,)), ((), ()))
NBIN = 256
LANES = 128
PACK = 16
X, Y, S = 0, 1, 2


def flip(c, bit):
    return c + bit - 2 * bit * lax.rem(lax.div(c, bit), 2)


def split(x, n):
    if n & (n - 1) == 0:
        return x >> (n.bit_length() - 1), x & (n - 1)
    return lax.div(x, n), lax.rem(x, n)


def body(rows, cols, x_ref, bins_ref, list_ref, members_ref, kern_ref, out_ref,
         subs_ref, xv, xf, bv, mv, kern, rowbuf, colbuf, bsend, bt, mid, msend, mirror, mt,
         member, pmask, hot0, hot1, cross0, cross1, w0, w1, acc, part, got1, spread, got2, ready, got3,
         in_sem, own_send, own_recv, fwd_send, fwd_recv, sib_send, sib_recv, col_send, col_recv,
         mid_send, mid_recv, mir_send, mir_recv, send1, recv1, send2, recv2, send3, recv3):
    r, c = lax.axis_index("row"), lax.axis_index("col")
    shard, freqs, _ = xv.shape
    span, width = bv.shape
    slots = subs_ref.shape[1]
    half = freqs // 2
    quarter = half // 2
    share = half // cols
    tiles = span // LANES
    per_tile = LANES // shard
    units = rows + 1
    tree = cols == 8 and tiles == 2
    own_tile = lax.div(c, per_tile)
    steps = rows + (tiles - 1) * (rows - 1) + tiles
    qa = jnp.where(2 * r < rows, 0, 1)
    qb = 1 - qa
    bf16, f32 = jnp.bfloat16, jnp.float32

    barrier = pltpu.get_barrier_semaphore()
    for d in range(1, rows):
        pl.semaphore_signal(barrier, inc=1, device_id=(lax.rem(r + d, rows), c), device_id_type=MESH)
    for d in range(1, cols):
        pl.semaphore_signal(barrier, inc=1, device_id=(r, lax.rem(c + d, cols)), device_id_type=MESH)
    loads = [pltpu.make_async_copy(bins_ref, bv, in_sem.at[0]),
             pltpu.make_async_copy(x_ref, xv, in_sem.at[1]),
             pltpu.make_async_copy(members_ref, mv, in_sem.at[2]),
             pltpu.make_async_copy(list_ref, subs_ref, in_sem.at[5])]
    fetches = [pltpu.make_async_copy(kern_ref.at[pl.ds(q * half + c * share, share)], kern.at[q], in_sem.at[3 + q])
               for q in range(2)]
    for copy in loads + fetches:
        copy.start()

    loads[0].wait()
    ids = bv[...].astype(f32)
    bsend[...] = ids.astype(bf16)
    mine = pl.ds(pl.multiple_of(c * shard, shard), shard)
    mid[c] = bsend[mine, :]
    loads[1].wait()
    xf[...] = xv[...].astype(f32).reshape(shard * freqs, xv.shape[2])
    for f in range(freqs):
        block = xf[pl.ds(f, shard, stride=freqs), :].astype(bf16)
        rowbuf[f, mine, :] = block
        if f < half:
            colbuf[r, f] = block
        else:
            colbuf[rows, f - half] = block

    def mid_copy(d):
        to = lax.rem(c + d, cols)
        return pltpu.make_async_remote_copy(
            bsend.at[pl.ds(pl.multiple_of(to * shard, shard), shard), :], mid.at[c], mid_send.at[d], mid_recv.at[d],
            device_id=(r, to), device_id_type=MESH)

    def mir_copy(d):
        to = lax.rem(r + d, rows)
        return pltpu.make_async_remote_copy(
            msend.at[to], mirror.at[r], mir_send.at[d], mir_recv.at[d], device_id=(to, c), device_id_type=MESH)

    def pick(q):
        return qb if q else qa

    def slot(index, q):
        return rowbuf.at[pl.ds(pick(q) * half, half), pl.ds(pl.multiple_of(index * shard, shard), shard), :]

    bits = (2, 4, 1)

    def own_copy(way, q):
        return pltpu.make_async_remote_copy(
            slot(c, q), slot(c, q), own_send.at[way, q], own_recv.at[way, q],
            device_id=(r, flip(c, bits[way])), device_id_type=MESH)

    def fwd_copy(q):
        source = flip(c, bits[X] if q == 0 else bits[Y])
        return pltpu.make_async_remote_copy(
            slot(source, q), slot(source, q), fwd_send.at[q], fwd_recv.at[q],
            device_id=(r, flip(c, bits[Y] if q == 0 else bits[X])), device_id_type=MESH)

    def sib_copy(k, q):
        source = (flip(c, 2), flip(c, 4), flip(flip(c, 2), 4))[k]
        return pltpu.make_async_remote_copy(
            slot(source, q), slot(source, q), sib_send.at[k, q], sib_recv.at[k, q],
            device_id=(r, flip(c, 1)), device_id_type=MESH)

    def direct_copy(d):
        place = rowbuf.at[:, mine, :]
        return pltpu.make_async_remote_copy(
            place, place, own_send.at[d, 0], own_recv.at[d, 0],
            device_id=(r, lax.rem(c + d, cols)), device_id_type=MESH)

    def col_copy(way, d, p):
        source = r - way * (d - 1)
        there = r + way
        at = lax.rem(source + rows, rows)
        if d == 1 and way > 0:
            at = rows
        place = colbuf.at[at, pl.ds(p * quarter, quarter)]
        target = colbuf.at[lax.rem(source + rows, rows), pl.ds(p * quarter, quarter)]
        i = (way + 1) // 2
        return (there >= 0) & (there < rows) & (source >= 0) & (source < rows), pltpu.make_async_remote_copy(
            place, target, col_send.at[i, d, p], col_recv.at[i, d, p],
            device_id=(lax.rem(there + rows, rows), c), device_id_type=MESH)

    def col_start(way, d, p):
        made = col_copy(way, d, p)
        pl.when(made[0])(made[1].start)

    def col_wait(way, d, p):
        source = r - way * d

        @pl.when((source >= 0) & (source < rows))
        def _():
            place = colbuf.at[lax.rem(source + rows, rows), pl.ds(p * quarter, quarter)]
            i = (way + 1) // 2
            pltpu.make_async_remote_copy(
                place, place, col_send.at[i, d, p], col_recv.at[i, d, p],
                device_id=(lax.rem(r + way + rows, rows), c), device_id_type=MESH).wait_recv()

    def col_pass(d):
        for p in range(2):
            for way in (1, -1):
                col_wait(way, d, p)
                if d < rows - 1:
                    col_start(way, d + 1, p)

    pl.semaphore_wait(barrier, cols + rows - 2)

    for d in range(1, cols):
        mid_copy(d).start()
    for p in range(2):
        for way in (1, -1):
            col_start(way, 1, p)
    if tree:
        own_copy(X, 0).start()
        own_copy(Y, 1).start()
        own_copy(X, 1).start()
        own_copy(Y, 0).start()
        own_copy(S, 0).start()
        own_copy(S, 1).start()
    else:
        for d in range(1, cols):
            direct_copy(d).start()

    loads[2].wait()
    loads[3].wait()
    stations = mv.shape[1]
    sub_at = lax.broadcasted_iota(jnp.int32, (slots, stations), 0)
    slot_ids = jnp.zeros((slots, stations), jnp.int32)
    for s in range(slots):
        slot_ids = jnp.where(sub_at == s, subs_ref[0, s], slot_ids)
    found = jnp.zeros((slots, stations), f32)
    for m in range(mv.shape[0]):
        found = jnp.where(slot_ids == mv[m:m + 1, :], 1.0, found)
    member[...] = found
    name = lax.broadcasted_iota(jnp.int32, (stations, width), 0)
    block_id, inside = split(lax.broadcasted_iota(jnp.int32, (stations, width), 1), shard)
    picked = jnp.where(name == (block_id * cols + c) * shard + inside, 1.0, 0.0).astype(bf16)
    col_mask = jnp.dot(found.astype(bf16), picked, preferred_element_type=f32)
    row_mask = member[:, pl.ds(pl.multiple_of(r * span, span), span)]
    lane = lax.broadcasted_iota(jnp.int32, (slots, width), 1)
    for t in range(tiles):
        bt[t] = ids[t * LANES:(t + 1) * LANES].T

    def bring(k, q):
        own_copy(k, q).wait_recv()
        if k == (X, Y)[q]:
            fwd_copy(q).start()
        sib_copy(k, q).start()

    def mask_one(j, carry):
        hit = jnp.sum(jnp.where(lane == j, col_mask, 0.0), axis=1, keepdims=True)
        pmask[j] = (hit * row_mask).astype(bf16)
        return carry

    lax.fori_loop(0, width, mask_one, 0, unroll=8)

    low = lax.broadcasted_iota(jnp.int32, (PACK, LANES), 0).astype(f32)
    levels = [(low + g * PACK).astype(bf16) for g in range(NBIN // PACK)]
    one, zero = jnp.ones((PACK, LANES), bf16), jnp.zeros((PACK, LANES), bf16)

    def spread_row(ref, index, t):
        row = ref[t, pl.ds(index, 1), :]
        return jnp.broadcast_to(row, (PACK, LANES)).astype(bf16)

    for d in range(1, cols):
        mid_copy(d).wait_recv()
    group = lax.broadcasted_iota(jnp.int32, (shard, LANES), 1) // shard
    for t in range(tiles):
        held = [mid[t * per_tile + k].astype(f32) for k in range(per_tile)]
        for b in range(rows):
            total = jnp.zeros((shard, LANES), f32)
            for k in range(per_tile):
                shift = ((k - b) * shard) % LANES
                moved = pltpu.roll(held[k], shift, 1) if shift else held[k]
                total = jnp.where(group == k, moved, total)
            msend[b, :, t * LANES:(t + 1) * LANES] = total.astype(bf16)
        mt[t, pl.ds(pl.multiple_of(r * shard, shard), shard), :] = jnp.where(
            own_tile == t, -1.0, msend[r, :, t * LANES:(t + 1) * LANES].astype(f32))
    for d in range(1, rows):
        mir_copy(d).start()

    col_pass(1)
    if tree:
        bring(X, 0)
        bring(Y, 1)
        own_copy(S, 0).wait_recv()
        sib_copy(X, 0).wait_recv()
    else:
        for d in range(1, cols):
            direct_copy(d).wait_recv()
    near = lax.min(r, rows - 1 - r)
    upward = jnp.where(r < rows - 1 - r, 1, -1)

    def unit_of(m):
        far = m >= steps - tiles
        first = m < rows
        t = jnp.where(far, m - (steps - tiles), jnp.where(first, 0, 1 + lax.div(lax.max(m - rows, 0), rows - 1)))
        u = jnp.where(far, rows, jnp.where(first, m, 1 + lax.rem(lax.max(m - rows, 0), rows - 1)))
        tile = lax.rem(own_tile + t, tiles)
        k = lax.max(u - 2, 0)
        paired = k < 2 * near
        way = jnp.where(paired, 1 - 2 * lax.rem(k, 2), upward)
        dist = jnp.where(paired, lax.div(k, 2) + 1, k - near + 1)
        other = r + way * dist
        block = jnp.where(u < 2, r, other)
        own_q = jnp.where(t == 0, jnp.where(u == 0, qa, qb), jnp.where(own_tile < tile, 0, 1))
        q = jnp.where(u < 2, own_q, jnp.where(way > 0, 0, 1))
        at = jnp.where((u < 2) & (q == 1), rows, block)
        return tile, block, q, at

    def need(m):
        if tree:
            @pl.when(m == 1)
            def _():
                bring(Y, 0)
                bring(X, 1)
                own_copy(S, 1).wait_recv()
                sib_copy(X, 1).wait_recv()

        @pl.when(m == 2)
        def _():
            for d in range(2, rows - 1):
                col_pass(d)
            for d in range(1, rows):
                mir_copy(d).wait_recv()
            for b in range(rows):
                @pl.when(b != r)
                def _():
                    for t in range(tiles):
                        mt[t, b * shard:(b + 1) * shard, :] = mirror[b, :, t * LANES:(t + 1) * LANES].astype(f32)

        if tree:
            @pl.when(m == rows)
            def _():
                for q in range(2):
                    fwd_copy(q).wait_recv()
                    sib_copy(2, q).start()
                for k in (1, 2):
                    for q in range(2):
                        sib_copy(k, q).wait_recv()

        @pl.when(m == steps - tiles)
        def _():
            for p in range(2):
                for way in (1, -1):
                    col_wait(way, rows - 1, p)

    def build(m, cross, w, hot):
        tile, block, q, at = unit_of(m)
        lanes = pl.ds(pl.multiple_of(tile * LANES, LANES), LANES)
        for f in range(half):
            cross[f * shard:(f + 1) * shard, :] = lax.dot_general(
                colbuf[at, f], rowbuf[q * half + f, lanes, :], NT, preferred_element_type=f32)
        for j in range(shard):
            here = spread_row(bt, block * shard + j, tile)
            there = spread_row(mt, block * shard + j, tile)
            for g, level in enumerate(levels):
                hot[j, g * PACK:(g + 1) * PACK, :] = (
                    jnp.where(here == level, one, zero) + jnp.where(there == level, one, zero))
            mask = pmask[block * shard + j, :, lanes]
            for f in range(half):
                value = jnp.broadcast_to(cross[f * shard + j:f * shard + j + 1, :], (slots, LANES)).astype(bf16)
                w[j, f * slots:(f + 1) * slots, :] = mask * value

    def multiply(m, w, hot):
        q = unit_of(m)[2]
        left = jnp.concatenate([w[j] for j in range(shard)], axis=1)
        right = jnp.concatenate([hot[j] for j in range(shard)], axis=1)
        acc[q] += lax.dot_general(left, right, NT, preferred_element_type=f32)

    acc[...] = jnp.zeros_like(acc)
    sets = ((cross0, w0, hot0), (cross1, w1, hot1))

    def advance(m, odd):
        build(m, *sets[odd])
        multiply(m - 1, *sets[1 - odd][1:])

    build(0, *sets[0])
    need(1)
    advance(1, 1)

    def two(i, carry):
        need(2 * i + 2)
        need(2 * i + 3)
        advance(2 * i + 2, 0)
        advance(2 * i + 3, 1)
        return carry

    depth = share * slots
    early = tiles == 2 and rows % 2 == 0

    def copy1(d, n):
        to = lax.rem(c + d, cols)
        return pltpu.make_async_remote_copy(
            part.at[to, pick(n)], got1.at[d, pick(n)], send1.at[d, n], recv1.at[d, n],
            device_id=(r, to), device_id_type=MESH)

    def hand_out(n):
        for k in range(cols):
            part[k, pick(n)] = acc[pick(n), k * depth:(k + 1) * depth, :].astype(bf16)
        for d in range(1, cols):
            copy1(d, n).start()

    paired = (steps - 2) // 2
    lax.fori_loop(0, paired, two, 0)
    if early:
        hand_out(1)
    if steps % 2:
        need(steps - 1)
        advance(steps - 1, 0)
    multiply(steps - 1, *sets[(steps - 1) % 2][1:])
    for n in range(1 if early else 2):
        hand_out(n)

    size = share * cols
    shape = (rows * size, depth)
    owner, tail = split(lax.broadcasted_iota(jnp.int32, shape, 0), size)
    fid, sid = split(tail, cols)
    fin, place = split(lax.broadcasted_iota(jnp.int32, shape, 1), slots)
    listed = jnp.zeros(shape, jnp.int32)
    for s in range(slots):
        listed = jnp.where(place == s, subs_ref[0, s], listed)
    chosen = jnp.where((owner * cols + sid == listed) & (fid == fin), 1.0, 0.0).astype(bf16)

    def copy2(d, n):
        to = lax.rem(r + d, rows)
        return pltpu.make_async_remote_copy(
            spread.at[to, pick(n)], got2.at[d, pick(n)], send2.at[d, n], recv2.at[d, n],
            device_id=(to, c), device_id_type=MESH)

    for n in (1, 0):
        for d in range(1, cols):
            copy1(d, n).wait_recv()
        total = part[c, pick(n)].astype(f32)
        for d in range(1, cols):
            total = total + got1[d, pick(n)].astype(f32)
        placed = jnp.dot(chosen, total.astype(bf16), preferred_element_type=f32).astype(bf16)
        for b in range(rows):
            spread[b, pick(n)] = placed[b * size:(b + 1) * size]
        for d in range(1, rows):
            copy2(d, n).start()
    for copy in fetches:
        copy.wait()
    for n in (1, 0):
        for d in range(1, rows):
            copy2(d, n).wait_recv()
    total = spread[r].astype(f32)
    for d in range(1, rows):
        total = total + got2[d].astype(f32)
    total = total.reshape(2 * size, NBIN)
    for q in range(2):
        for f in range(share):
            n = q * share + f
            power = jnp.dot(total[n * cols:(n + 1) * cols].astype(bf16), kern[q, f], preferred_element_type=f32)
            power = power * lax.rsqrt(jnp.mean(power * power, axis=1, keepdims=True) + 1e-06)
            for k in range(cols):
                ready[k, n:n + 1, :] = power[k:k + 1]

    def copy3(d):
        to = lax.rem(c + d, cols)
        return pltpu.make_async_remote_copy(
            ready.at[to], got3.at[d], send3.at[d], recv3.at[d], device_id=(r, to), device_id_type=MESH)

    def put(source, block):
        for q in range(2):
            for f in range(share):
                out_ref[0, pl.ds(q * half + source * share + f, 1), :] = block[q * share + f:q * share + f + 1]

    for d in range(1, cols):
        copy3(d).start()
    put(c, ready[c])
    for d in range(1, cols):
        copy3(d).wait_recv()
        put(lax.rem(c - d + cols, cols), got3[d])
    for d in range(1, cols):
        mid_copy(d).wait_send()
        copy1(d, 0).wait_send()
        copy1(d, 1).wait_send()
        copy3(d).wait_send()
    for d in range(1, rows):
        mir_copy(d).wait_send()
        copy2(d, 0).wait_send()
        copy2(d, 1).wait_send()
        for p in range(2):
            for way in (1, -1):
                made = col_copy(way, d, p)
                pl.when(made[0])(made[1].wait_send)
    if tree:
        for q in range(2):
            for k in range(3):
                own_copy(k, q).wait_send()
                sib_copy(k, q).wait_send()
            fwd_copy(q).wait_send()
    else:
        for d in range(1, cols):
            direct_copy(d).wait_send()


def on_device(spectra, pair_bins, row_subs, station_subs, kernel):
    shard, freqs, width = spectra.shape
    rows, cols = lax.axis_size("row"), lax.axis_size("col")
    span, group = pair_bins.shape
    slots = row_subs.shape[1]
    half = freqs // 2
    share = half // cols
    depth = share * slots
    size = share * cols
    speeds = kernel.shape[2]
    tiles = span // LANES
    dma = pltpu.SemaphoreType.DMA
    bf16, f32 = jnp.bfloat16, jnp.float32
    hbm = pl.BlockSpec(memory_space=pl.ANY)
    return pl.pallas_call(
        functools.partial(body, rows, cols),
        out_shape=jax.ShapeDtypeStruct((1, freqs, speeds), f32),
        in_specs=[hbm] * 5,
        out_specs=pl.BlockSpec(memory_space=pltpu.VMEM),
        scratch_shapes=[
            pltpu.SMEM((1, slots), jnp.int32),
            pltpu.VMEM(spectra.shape, bf16),
            pltpu.VMEM((shard * freqs, width), f32),
            pltpu.VMEM((span, group), jnp.int32),
            pltpu.VMEM((station_subs.shape[1], station_subs.shape[0]), jnp.int32),
            pltpu.VMEM((2, share, NBIN, speeds), bf16),
            pltpu.VMEM((freqs, cols * shard, width), bf16),
            pltpu.VMEM((rows + 1, half, shard, width), bf16),
            pltpu.VMEM((span, group), bf16),
            pltpu.VMEM((tiles, group, LANES), f32),
            pltpu.VMEM((cols, shard, group), bf16),
            pltpu.VMEM((rows, shard, span), bf16),
            pltpu.VMEM((rows, shard, span), bf16),
            pltpu.VMEM((tiles, group, LANES), f32),
            pltpu.VMEM((slots, station_subs.shape[0]), f32),
            pltpu.VMEM((group, slots, span), bf16),
            pltpu.VMEM((shard, NBIN, LANES), bf16),
            pltpu.VMEM((shard, NBIN, LANES), bf16),
            pltpu.VMEM((half * shard, LANES), f32),
            pltpu.VMEM((half * shard, LANES), f32),
            pltpu.VMEM((shard, half * slots, LANES), bf16),
            pltpu.VMEM((shard, half * slots, LANES), bf16),
            pltpu.VMEM((2, half * slots, NBIN), f32),
            pltpu.VMEM((cols, 2, depth, NBIN), bf16),
            pltpu.VMEM((cols, 2, depth, NBIN), bf16),
            pltpu.VMEM((rows, 2, size, NBIN), bf16),
            pltpu.VMEM((rows, 2, size, NBIN), bf16),
            pltpu.VMEM((cols, 2 * share, speeds), f32),
            pltpu.VMEM((cols, 2 * share, speeds), f32),
            dma((6,)),
            dma((cols, 2)), dma((cols, 2)), dma((2,)), dma((2,)), dma((3, 2)), dma((3, 2)),
            dma((2, rows, 2)), dma((2, rows, 2)),
            dma((cols,)), dma((cols,)), dma((rows,)), dma((rows,)),
            dma((cols, 2)), dma((cols, 2)), dma((rows, 2)), dma((rows, 2)), dma((cols,)), dma((cols,)),
        ],
        compiler_params=pltpu.CompilerParams(collective_id=0, has_side_effects=True, vmem_limit_bytes=62 << 20),
        name="dispersion",
    )(spectra, pair_bins, row_subs, station_subs.T, kernel)


def solution(mesh):
    in_specs = (P(("row", "col"), None, None), P("row", "col"), P("row", None), P(), P())
    out_specs = P(("row", "col"), None, None)
    return jax.shard_map(
        on_device, mesh=mesh, in_specs=in_specs, out_specs=out_specs, check_vma=False
    )
```
